768 devices in a mesh: row: 96 (over y_lo, z, core), col: 8 (over x, y_hi).
Axes of the slice: x: 4, y: 8 (y_hi: 2, y_lo: 4; y = y_hi * 4 + y_lo), z: 12, core: 2. Of those that a mesh axis runs over, the one named last changes fastest.
Arguments:
- static_design: bfloat16 [1536, 24576], P('col', 'row'), may hold values from -6 to 6
- tv_design: bfloat16 [1536, 24576], P('row', 'col'), may hold values from -0.15625 to 0.15625
- taps: float32 [32], replicated, may hold values from -1 to 1
- arc_id: int32 [1536], replicated, may hold values from 0 to 3, never falling along the last dimension, each value on 1 to 768 neighbouring positions
Outputs:
- normal_block: float32 [24576, 24576], P('row', 'col')
The draws below stay inside these ranges and needn't reach their ends.
Inputs may be any that keep to these rules, and one draw needn't show every extreme that they name: `arc_id`: arc numbers never fall along the rows; each arc has 1 to 768 rows and one has exactly 768.
All inputs are finite; a program needn't handle non-finite values.
Results may differ from the reference program's by a relative error of at most 0.0029.
Values may be sent and summed in bfloat16 or wider, within the bound.
No kernel may reach another device: no remote copies, remote signals or barrier semaphores. Data moves between devices by JAX's collectives and lax.ppermute only.
A program may use at most 64 MiB of HBM per device.

```python
import math
import jax
import jax.numpy as jnp
import numpy as np
from jax import lax

TAPS = 32
ARCS = 4
S = 24576
TV = 24576
R = 1536
ARC_MOST = 768


def level_of(rng, shape, cuts, low, largest):
    def one(axis_at, blocks):
        heights = jax.random.uniform(jax.random.fold_in(jax.random.fold_in(rng, 6), axis_at), (blocks,), jnp.float32, low / len(cuts), largest / len(cuts))
        return jnp.repeat(jnp.exp(heights), shape[axis_at] // blocks).reshape((-1,) + (1,) * (len(shape) - axis_at - 1))

    factor_of = one(*cuts[0])
    for cut in cuts[1:]:
        factor_of = factor_of * one(*cut)
    return factor_of


def profile(count, total, bound, skew):
    portions = [(1 << 20) // math.isqrt(rank ** skew) + 1 for rank in range(2, count + 1)]
    surplus, given = total - bound - (count - 1), [1] * (count - 1)
    while surplus > 0:
        movable = [i for i in range(count - 1) if given[i] < bound]
        mass, left = sum([portions[i] for i in movable]), surplus
        for i in movable:
            addition = min(bound - given[i], max(1, left * portions[i] // mass), surplus)
            given[i] = given[i] + addition
            surplus = surplus - addition
    return np.array([bound] + given)


def ragged(rng, number_of, total, bound, skew):
    if number_of == 2:
        one = jax.random.randint(rng, (), max(1, total - bound), min(bound, total - 1) + 1)
        return jnp.stack([one, total - one])
    sizes = jnp.asarray(profile(number_of, total, bound, skew), jnp.int32)
    pairs = (number_of - 1) // 2
    donor, receiver = sizes[1:1 + 2 * pairs:2], sizes[2:2 + 2 * pairs:2]
    slack = jnp.minimum(donor - 1, bound - receiver)
    passed = jax.random.randint(jax.random.fold_in(rng, 1), (pairs,), 0, 1 << 20) % (slack + 1)
    sizes = sizes.at[1:1 + 2 * pairs:2].set(donor - passed).at[2:2 + 2 * pairs:2].set(receiver + passed)
    return sizes[jax.random.permutation(jax.random.fold_in(rng, 2), number_of)]


def bell_draw(stream_key, shape, spread, bound, pieces=(), dtype=jnp.bfloat16):
    entries = spread * jax.random.normal(stream_key, shape, jnp.float32)
    if pieces:
        entries = entries * level_of(stream_key, shape, pieces, -0.22, 0.18)
    return jnp.clip(entries, -bound, bound).astype(dtype)


def setup_inputs(seed: int = 0) -> dict:
    key_list = jax.random.split(jax.random.key(seed), 5)
    return {
        "static_design": bell_draw(key_list[0], (R, S), 1.0, 6.0, ((0, 8), (1, 96))),
        "tv_design": bell_draw(key_list[1], (R, TV), R ** -0.5, 0.15625, ((0, 96), (1, 8))),
        "taps": bell_draw(key_list[2], (TAPS,), 0.18, 1.0, (), jnp.float32),
        "arc_id": jnp.searchsorted(jnp.cumsum(ragged(key_list[3], ARCS, R, ARC_MOST, 0)), jnp.arange(R), side="right").astype(jnp.int32),
    }


def shift_down(values, steps, fill):
    pads = [(steps, 0)] + [(0, 0)] * (values.ndim - 1)
    return jnp.pad(values, pads, constant_values=fill)[: values.shape[0]]


def shift_up(values, steps, fill):
    pads = [(0, steps)] + [(0, 0)] * (values.ndim - 1)
    return jnp.pad(values, pads, constant_values=fill)[steps:]


def decorrelate(block, arcs, taps):
    count = taps.shape[0]
    forward = jnp.zeros(block.shape, jnp.float32)
    for step in range(count):
        same = (shift_down(arcs, step, -2) == arcs)[:, None]
        forward = forward + taps[step] * jnp.where(same, shift_down(block, step, 0.0), 0.0)
    backward = jnp.zeros(block.shape, jnp.float32)
    for step in range(count):
        same = (shift_up(arcs, step, -2) == arcs)[:, None]
        backward = backward + taps[step] * jnp.where(same, shift_up(forward, step, 0.0), 0.0)
    return backward


def reference(static_design, tv_design, taps, arc_id):
    edge = taps.shape[0] - 1
    block = jnp.pad(static_design.astype(jnp.float32), ((edge, edge), (0, 0)))
    arcs = jnp.pad(arc_id, (edge, edge), constant_values=-1)
    weighted = decorrelate(block, arcs, taps)[edge:-edge].astype(jnp.bfloat16)
    return lax.dot_general(weighted, tv_design, (((0,), (0,)), ((), ())), preferred_element_type=jnp.float32)
```

```python
import functools

import jax
import jax.numpy as jnp
from jax import lax
from jax.experimental import pallas as pl
from jax.experimental.pallas import tpu as pltpu
from jax.sharding import Mesh
from jax.sharding import PartitionSpec as P

BLOCK = 256
EDGE = 32
COL = ("col_0", "col_1")


def split(values, parts):
    pieces = []
    for _ in range(parts):
        piece = values.astype(jnp.bfloat16)
        pieces.append(piece)
        values = values - piece.astype(jnp.float32)
    return pieces


def banded(taps, lag):
    band = jnp.zeros(lag.shape, jnp.float32)
    for step in range(taps.shape[0]):
        band = jnp.where(lag == step, taps[step], band)
    return band


def weigh(groups, taps, arc_rows, arc_ahead, arc_behind, static, out, padded, *filtered):
    rows, width = static.shape
    wide = BLOCK + EDGE
    down = lax.broadcasted_iota(jnp.int32, (BLOCK, wide), 0)
    across = lax.broadcasted_iota(jnp.int32, (BLOCK, wide), 1)
    forward = banded(taps, down + EDGE - across)
    backward = banded(taps, across - down)

    padded[:EDGE] = jnp.zeros((EDGE, width), padded.dtype)
    padded[EDGE:] = static[...]
    for piece in filtered:
        piece[rows:] = jnp.zeros((EDGE, width), piece.dtype)
    dot = functools.partial(jnp.dot, preferred_element_type=jnp.float32)
    for start in range(0, rows, BLOCK):
        same = arc_rows[start : start + BLOCK] == arc_behind[:, start : start + wide]
        window = padded[start : start + wide]
        total = jnp.zeros((BLOCK, width), jnp.float32)
        for piece in split(jnp.where(same, forward, 0.0), 3)[::-1]:
            total = total + dot(piece, window)
        for ref, piece in zip(filtered, split(total, 3), strict=True):
            ref[start : start + BLOCK] = piece
    per = rows // groups // 16
    for start in range(0, rows, BLOCK):
        same = arc_rows[start : start + BLOCK] == arc_ahead[:, start : start + wide]
        pieces = split(jnp.where(same, backward, 0.0), 3)
        total = jnp.zeros((BLOCK, width), jnp.float32)
        for i, j in ((2, 0), (1, 1), (0, 2), (1, 0), (0, 1), (0, 0)):
            total = total + dot(pieces[i], filtered[j][start : start + wide])
        total = total.astype(out.dtype)
        for tile in range(BLOCK // 16):
            group, place = divmod(start // 16 + tile, per)
            at = (place * groups + group) * 16
            out[at : at + 16] = total[tile * 16 : tile * 16 + 16]


def weighted(static, taps, arc_id, groups):
    rows, width = static.shape
    spare = (0, 128 - EDGE)
    arc_behind = jnp.pad(arc_id, (EDGE, 0), constant_values=-1)
    arc_behind = jnp.pad(arc_behind, spare, constant_values=-1)[None]
    arc_ahead = jnp.pad(arc_id, (0, 128), constant_values=-1)[None]
    vmem = pl.BlockSpec(memory_space=pltpu.VMEM)
    return pl.pallas_call(
        functools.partial(weigh, groups),
        out_shape=jax.ShapeDtypeStruct((rows, width), jnp.bfloat16),
        in_specs=[pl.BlockSpec(memory_space=pltpu.SMEM)] + [vmem] * 4,
        out_specs=vmem,
        scratch_shapes=[pltpu.VMEM((rows + EDGE, width), jnp.bfloat16)] * 4,
        cost_estimate=pl.CostEstimate(
            flops=18 * rows * (BLOCK + EDGE) * width,
            bytes_accessed=4 * rows * width,
            transcendentals=0,
        ),
    )(taps, arc_id[:, None], arc_ahead, arc_behind, static)


def body(static_design, tv_design, taps, arc_id):
    short = lax.all_gather(tv_design, "short", axis=0, tiled=True)
    whole_tv = lax.all_gather(short, ("ring", "core"), axis=0, tiled=True)
    whole_static = static_design
    for axis in reversed(COL):
        whole_static = lax.all_gather(whole_static, axis, axis=0, tiled=True)
    left = weighted(whole_static, taps, arc_id, lax.axis_size("short"))
    contract = (((0,), (0,)), ((), ()))
    return lax.dot_general(left, whole_tv, contract, preferred_element_type=jnp.float32)


def solution(mesh):
    finer = Mesh(
        mesh.devices.reshape(4, 12, 2, 4, 2),
        ("short", "ring", "core", "col_0", "col_1"),
    )
    row = ("short", "ring", "core")
    placed = (P(COL, row), P(row, COL), P(), P())
    return jax.shard_map(
        body, mesh=finer, in_specs=placed, out_specs=P(row, COL), check_vma=False
    )
```

```python
import functools

import jax
import jax.numpy as jnp
from jax import lax
from jax.experimental import pallas as pl
from jax.experimental.pallas import tpu as pltpu
from jax.sharding import Mesh
from jax.sharding import PartitionSpec as P

BLOCK = 256
EDGE = 32
COL = ("col_0", "col_1")


def split(values, parts):
    pieces = []
    for _ in range(parts):
        piece = values.astype(jnp.bfloat16)
        pieces.append(piece)
        values = values - piece.astype(jnp.float32)
    return pieces


def banded(taps, lag):
    band = jnp.zeros(lag.shape, jnp.float32)
    for step in range(taps.shape[0]):
        band = jnp.where(lag == step, taps[step], band)
    return band


def weigh(groups, turns, place, taps, arc_rows, arc_ahead, arc_behind, *refs):
    pairs, (out, padded, *filtered) = refs[: len(turns)], refs[len(turns) :]
    rows, width = out.shape
    wide = BLOCK + EDGE
    down = lax.broadcasted_iota(jnp.int32, (BLOCK, wide), 0)
    across = lax.broadcasted_iota(jnp.int32, (BLOCK, wide), 1)
    forward = banded(taps, down + EDGE - across)
    backward = banded(taps, across - down)

    padded[:EDGE] = jnp.zeros((EDGE, width), padded.dtype)
    for turn, pair in zip(turns, pairs, strict=True):
        own = pair.shape[1]
        for j in range(2):
            block = lax.rem(place[0] + turn, 4) * 2 + (place[1] + j) % 2
            at = pl.multiple_of(EDGE + block * own, 32)
            padded[pl.ds(at, own)] = pair[j]
    for piece in filtered:
        piece[rows:] = jnp.zeros((EDGE, width), piece.dtype)
    dot = functools.partial(jnp.dot, preferred_element_type=jnp.float32)
    for start in range(0, rows, BLOCK):
        same = arc_rows[start : start + BLOCK] == arc_behind[:, start : start + wide]
        window = padded[start : start + wide]
        total = jnp.zeros((BLOCK, width), jnp.float32)
        for piece in split(jnp.where(same, forward, 0.0), 3)[::-1]:
            total = total + dot(piece, window)
        for ref, piece in zip(filtered, split(total, 3), strict=True):
            ref[start : start + BLOCK] = piece
    per = rows // groups // 16
    for start in range(0, rows, BLOCK):
        same = arc_rows[start : start + BLOCK] == arc_ahead[:, start : start + wide]
        pieces = split(jnp.where(same, backward, 0.0), 3)
        total = jnp.zeros((BLOCK, width), jnp.float32)
        for i, j in ((2, 0), (1, 1), (0, 2), (1, 0), (0, 1), (0, 0)):
            total = total + dot(pieces[i], filtered[j][start : start + wide])
        total = total.astype(out.dtype)
        for tile in range(BLOCK // 16):
            group, spot = divmod(start // 16 + tile, per)
            at = (spot * groups + group) * 16
            out[at : at + 16] = total[tile * 16 : tile * 16 + 16]


SMEM = pl.BlockSpec(memory_space=pltpu.SMEM)
VMEM = pl.BlockSpec(memory_space=pltpu.VMEM)


def weighted(place, pairs, turns, taps, arc_id, groups):
    width = pairs[0].shape[-1]
    rows = arc_id.shape[0]
    arc_behind = jnp.pad(arc_id, (EDGE, 128 - EDGE), constant_values=-1)[None]
    arc_ahead = jnp.pad(arc_id, (0, 128), constant_values=-1)[None]
    return pl.pallas_call(
        functools.partial(weigh, groups, turns),
        out_shape=jax.ShapeDtypeStruct((rows, width), jnp.bfloat16),
        in_specs=[SMEM, SMEM] + [VMEM] * (3 + len(pairs)),
        out_specs=VMEM,
        scratch_shapes=[pltpu.VMEM((rows + EDGE, width), jnp.bfloat16)] * 4,
        compiler_params=pltpu.CompilerParams(vmem_limit_bytes=16 << 20),
        cost_estimate=pl.CostEstimate(
            flops=18 * rows * (BLOCK + EDGE) * width,
            bytes_accessed=4 * rows * width,
            transcendentals=0,
        ),
    )(place, taps, arc_id[:, None], arc_ahead, arc_behind, *pairs)


def accumulate(hops, sides, carried, spot, *refs):
    weights, refs = refs[:sides], refs[sides:]
    blocks, refs = refs[: len(hops)], refs[len(hops) :]
    priors, outs, left = refs[:carried], refs[carried : carried + sides], refs[-1]
    z, core = spot[0], spot[1]
    half = weights[0].shape[0] // 24

    @pl.when(pl.program_id(0) == 0)
    def _():
        for side in range(sides):
            picked = []
            for (hop, part), block in zip(hops, blocks, strict=True):
                origin = lax.rem(z + jnp.where(core == 0, 12 - hop, hop), 12)
                at = origin * 2 if part == 2 else origin * 2 + (core + part) % 2
                rows = pl.ds(pl.multiple_of(at * half, half), block.shape[0])
                picked.append(weights[side][rows])
            left[side] = jnp.concatenate(picked, axis=0).T

    right = jnp.concatenate([block[...] for block in blocks], axis=0)
    for side in range(sides):
        total = jnp.dot(left[side], right, preferred_element_type=jnp.float32)
        for prior in priors[side::sides]:
            total = total + prior[...]
        outs[side][...] = total


def product(spot, weights, blocks, hops, priors, tile):
    sides = len(weights)
    depth = sum(block.shape[0] for block in blocks)
    columns = blocks[0].shape[1]
    width = weights[0].shape[1]
    spec = pl.BlockSpec((width, tile), lambda i: (0, i))
    return pl.pallas_call(
        functools.partial(accumulate, hops, sides, len(priors)),
        out_shape=[jax.ShapeDtypeStruct((width, columns), jnp.float32)] * sides,
        grid=(columns // tile,),
        in_specs=[SMEM]
        + [VMEM] * sides
        + [pl.BlockSpec((b.shape[0], tile), lambda i: (0, i)) for b in blocks]
        + [spec] * len(priors),
        out_specs=[spec] * sides,
        scratch_shapes=[pltpu.VMEM((sides, width, depth), jnp.bfloat16)],
        compiler_params=pltpu.CompilerParams(vmem_limit_bytes=16 << 20),
        cost_estimate=pl.CostEstimate(
            flops=2 * sides * width * depth * columns,
            bytes_accessed=2 * depth * columns + 4 * (sides + len(priors)) * width * columns,
            transcendentals=0,
        ),
    )(spot, *weights, *blocks, *priors)


def block_of(static_design, tv_design, taps, arc_id):
    turns = lax.axis_size("ring")
    half = turns // 2
    spot = jnp.stack([lax.axis_index("ring"), lax.axis_index("core")])
    place = jnp.stack([lax.axis_index("col_0"), lax.axis_index("col_1")])
    swap = [(0, 1), (1, 0)]
    onward = [(2 * i, (i + 1) % turns * 2) for i in range(turns)]
    onward += [((i + 1) % turns * 2 + 1, i * 2 + 1) for i in range(turns)]

    def hop(block):
        return lax.ppermute(block, ("ring", "core"), onward)

    other = lax.ppermute(static_design, "col_1", swap)
    mine = [lax.all_gather(tv_design, "short", axis=0, tiled=True)]
    theirs = [lax.ppermute(mine[0], "core", swap)]

    pair = jnp.stack([static_design, other])
    steps = (1, 3, 2)
    pairs = [pair]
    for step in steps:
        pairs.append(lax.ppermute(pair, "col_0", [((i + step) % 4, i) for i in range(4)]))
    for _ in range(1, half):
        mine.append(hop(mine[-1]))
        theirs.append(hop(theirs[-1]))
    mine.append(hop(mine[-1]))

    left = weighted(place, pairs, (0,) + steps, taps, arc_id, lax.axis_size("short"))
    lefts = (left, lax.ppermute(left, "core", swap))

    def both(first, last):
        blocks = [mine[d] for d in range(first, last)]
        hops = [(d, 0) for d in range(first, last)]
        for d in range(max(first, 1), last):
            blocks.append(theirs[d])
            hops.append((d, 1))
        return blocks, tuple(hops)

    sums = product(spot, lefts, *both(0, 4), (), 512)
    sums = product(spot, lefts, *both(4, half), sums, 512)
    handed = lax.ppermute(sums[1], "core", swap)
    far = lax.all_gather(mine[half], "core", axis=0, tiled=True)
    return product(spot, lefts[:1], [far], ((half, 2),), (sums[0], handed), 512)[0]


def solution(mesh):
    finer = Mesh(
        mesh.devices.reshape(4, 12, 2, 4, 2),
        ("short", "ring", "core", "col_0", "col_1"),
    )
    row = ("short", "ring", "core")
    placed = (P(COL, row), P(row, COL), P(), P())
    return jax.shard_map(
        block_of, mesh=finer, in_specs=placed, out_specs=P(row, COL), check_vma=False
    )
```

```python
import functools

import jax
import jax.numpy as jnp
from jax import lax
from jax.experimental import pallas as pl
from jax.experimental.pallas import tpu as pltpu
from jax.sharding import Mesh
from jax.sharding import PartitionSpec as P

BLOCK = 192
EDGE = 32
COL = ("col_0", "col_1")


def split(values, parts):
    pieces = []
    for _ in range(parts):
        piece = values.astype(jnp.bfloat16)
        pieces.append(piece)
        values = values - piece.astype(jnp.float32)
    return pieces


def banded(taps, lag):
    band = jnp.zeros(lag.shape, jnp.float32)
    for step in range(taps.shape[0]):
        band = jnp.where(lag == step, taps[step], band)
    return band


def weigh(groups, places, taps, arc_rows, arc_ahead, arc_behind, *refs):
    stacks, (out, padded, *filtered) = refs[:3], refs[3:]
    rows, width = out.shape
    wide = BLOCK + EDGE
    down = lax.broadcasted_iota(jnp.int32, (BLOCK, wide), 0)
    across = lax.broadcasted_iota(jnp.int32, (BLOCK, wide), 1)
    forward = banded(taps, down + EDGE - across)
    backward = banded(taps, across - down)

    padded[:EDGE] = jnp.zeros((EDGE, width), padded.dtype)
    blocks = [(stack, i) for stack in stacks for i in range(stack.shape[0])]
    for number, (stack, i) in enumerate(blocks):
        own = stack.shape[1]
        at = pl.multiple_of(EDGE + places[number] * own, 32)
        padded[pl.ds(at, own)] = stack[i]
    for piece in filtered:
        piece[rows:] = jnp.zeros((EDGE, width), piece.dtype)
    dot = functools.partial(jnp.dot, preferred_element_type=jnp.float32)
    for start in range(0, rows, BLOCK):
        same = arc_rows[start : start + BLOCK] == arc_behind[:, start : start + wide]
        window = padded[start : start + wide]
        total = jnp.zeros((BLOCK, width), jnp.float32)
        for piece in split(jnp.where(same, forward, 0.0), 3)[::-1]:
            total = total + dot(piece, window)
        for ref, piece in zip(filtered, split(total, 3), strict=True):
            ref[start : start + BLOCK] = piece
    per = rows // groups // 16
    for start in range(0, rows, BLOCK):
        same = arc_rows[start : start + BLOCK] == arc_ahead[:, start : start + wide]
        pieces = split(jnp.where(same, backward, 0.0), 3)
        total = jnp.zeros((BLOCK, width), jnp.float32)
        for i, j in ((2, 0), (1, 1), (0, 2), (1, 0), (0, 1), (0, 0)):
            total = total + dot(pieces[i], filtered[j][start : start + wide])
        total = total.astype(out.dtype)
        for tile in range(BLOCK // 16):
            group, spot = divmod(start // 16 + tile, per)
            at = (spot * groups + group) * 16
            out[at : at + 16] = total[tile * 16 : tile * 16 + 16]


SMEM = pl.BlockSpec(memory_space=pltpu.SMEM)
VMEM = pl.BlockSpec(memory_space=pltpu.VMEM)


def weighted(places, stacks, taps, arc_id, groups):
    width = stacks[0].shape[-1]
    rows = arc_id.shape[0]
    arc_behind = jnp.pad(arc_id, (EDGE, 128 - EDGE), constant_values=-1)[None]
    arc_ahead = jnp.pad(arc_id, (0, 128), constant_values=-1)[None]
    return pl.pallas_call(
        functools.partial(weigh, groups),
        out_shape=jax.ShapeDtypeStruct((rows, width), jnp.bfloat16),
        in_specs=[SMEM, SMEM] + [VMEM] * (3 + len(stacks)),
        out_specs=VMEM,
        scratch_shapes=[pltpu.VMEM((rows + EDGE, width), jnp.bfloat16)] * 4,
        compiler_params=pltpu.CompilerParams(vmem_limit_bytes=16 << 20),
        cost_estimate=pl.CostEstimate(
            flops=18 * rows * (BLOCK + EDGE) * width,
            bytes_accessed=4 * rows * width,
            transcendentals=0,
        ),
    )(places, taps, arc_id[:, None], arc_ahead, arc_behind, *stacks)


def accumulate(count, sides, carried, at, *refs):
    weights, refs = refs[:sides], refs[sides:]
    blocks, refs = refs[:count], refs[count:]
    priors, outs, left = refs[:carried], refs[carried : carried + sides], refs[-1]
    half = weights[0].shape[0] // 24

    @pl.when(pl.program_id(0) == 0)
    def _():
        for side in range(sides):
            picked = []
            for number in range(left.shape[2] // half):
                rows = pl.ds(pl.multiple_of(at[number] * half, half), half)
                picked.append(weights[side][rows])
            left[side] = jnp.concatenate(picked, axis=0).T

    right = jnp.concatenate([block[...] for block in blocks], axis=0)
    for side in range(sides):
        total = jnp.dot(left[side], right, preferred_element_type=jnp.float32)
        for prior in priors[side::sides]:
            total = total + prior[...]
        outs[side][...] = total


def product(at, weights, blocks, priors, tile):
    sides = len(weights)
    depth = sum(block.shape[0] for block in blocks)
    columns = blocks[0].shape[1]
    width = weights[0].shape[1]
    spec = pl.BlockSpec((width, tile), lambda i: (0, i))
    return pl.pallas_call(
        functools.partial(accumulate, len(blocks), sides, len(priors)),
        out_shape=[jax.ShapeDtypeStruct((width, columns), jnp.float32)] * sides,
        grid=(columns // tile,),
        in_specs=[SMEM]
        + [VMEM] * sides
        + [pl.BlockSpec((b.shape[0], tile), lambda i: (0, i)) for b in blocks]
        + [spec] * len(priors),
        out_specs=[spec] * sides,
        scratch_shapes=[pltpu.VMEM((sides, width, depth), jnp.bfloat16)],
        compiler_params=pltpu.CompilerParams(vmem_limit_bytes=16 << 20),
        cost_estimate=pl.CostEstimate(
            flops=2 * sides * width * depth * columns,
            bytes_accessed=2 * depth * columns + 4 * (sides + len(priors)) * width * columns,
            transcendentals=0,
        ),
    )(at, *weights, *blocks, *priors)


def block_of(static_design, tv_design, taps, arc_id):
    turns = lax.axis_size("ring")
    half = turns // 2
    ring, core = lax.axis_index("ring"), lax.axis_index("core")
    swap = [(0, 1), (1, 0)]
    onward = [(2 * i, (i + 1) % turns * 2) for i in range(turns)]
    onward += [((i + 1) % turns * 2 + 1, i * 2 + 1) for i in range(turns)]

    def hop(block):
        return lax.ppermute(block, ("ring", "core"), onward)

    other = lax.ppermute(static_design, "col_1", swap)
    mine = [lax.all_gather(tv_design, "short", axis=0, tiled=True)]
    theirs = [lax.ppermute(mine[0], "core", swap)]

    pair = jnp.stack([static_design, other])
    beside = lax.ppermute(pair, "col_0", [(i, i ^ 1) for i in range(4)])
    opposite = lax.ppermute(jnp.concatenate([pair, beside]), "col_0", [(i, 3 - i) for i in range(4)])
    places = (lax.axis_index("col_0") ^ jnp.array([0, 0, 1, 1, 3, 3, 2, 2], jnp.int32)) * 2
    places = places + (lax.axis_index("col_1") ^ jnp.array([0, 1] * 4, jnp.int32))

    for _ in range(1, half):
        mine.append(hop(mine[-1]))
        theirs.append(hop(theirs[-1]))
    mine.append(hop(mine[-1]))

    left = weighted(places, (pair, beside, opposite), taps, arc_id, lax.axis_size("short"))
    lefts = (left, lax.ppermute(left, "core", swap))

    def chosen(blocks):
        part = jnp.array([part for part, _ in blocks], jnp.int32)
        steps = jnp.array([steps for _, steps in blocks], jnp.int32)
        origin = (ring + turns + jnp.where(core == 0, -steps, steps)) % turns
        return origin * 2 + (core + part) % 2

    def near(blocks, priors):
        tv = [(mine, theirs)[part][steps] for part, steps in blocks]
        return product(chosen(blocks), lefts, tv, priors, 512)

    sums = near([(0, d) for d in range(4)] + [(1, d) for d in range(1, 4)], ())
    sums = near([(0, 4), (1, 4), (0, 5)], sums)
    handed = lax.ppermute(sums[1], "core", swap)
    far = [lax.all_gather(theirs[half - 1], "core", axis=0, tiled=True)]
    far.append(lax.all_gather(mine[half], "core", axis=0, tiled=True))
    steps = jnp.array([1 - half, half - 1, -half, half], jnp.int32)
    at = (ring + turns + steps) % turns * 2 + jnp.array([1, 0, 0, 1], jnp.int32)
    return product(at, lefts[:1], far, (sums[0], handed), 512)[0]


def solution(mesh):
    finer = Mesh(
        mesh.devices.reshape(4, 12, 2, 4, 2),
        ("short", "ring", "core", "col_0", "col_1"),
    )
    row = ("short", "ring", "core")
    placed = (P(COL, row), P(row, COL), P(), P())
    return jax.shard_map(
        block_of, mesh=finer, in_specs=placed, out_specs=P(row, COL), check_vma=False
    )
```

```python
import functools

import jax
import jax.numpy as jnp
from jax import lax
from jax.experimental import pallas as pl
from jax.experimental.pallas import tpu as pltpu
from jax.sharding import Mesh
from jax.sharding import PartitionSpec as P

BLOCK = 192
EDGE = 32
COL = ("col_0", "col_1")


def split(values, parts):
    pieces = []
    for _ in range(parts):
        piece = values.astype(jnp.bfloat16)
        pieces.append(piece)
        values = values - piece.astype(jnp.float32)
    return pieces


def banded(taps, lag):
    band = jnp.zeros(lag.shape, jnp.float32)
    for step in range(taps.shape[0]):
        band = jnp.where(lag == step, taps[step], band)
    return band


def weigh(groups, places, taps, arc_rows, arc_ahead, arc_behind, *refs):
    stacks, (out, padded, *filtered) = refs[:3], refs[3:]
    rows, width = out.shape
    wide = BLOCK + EDGE
    down = lax.broadcasted_iota(jnp.int32, (BLOCK, wide), 0)
    across = lax.broadcasted_iota(jnp.int32, (BLOCK, wide), 1)
    forward = banded(taps, down + EDGE - across)
    backward = banded(taps, across - down)

    padded[:EDGE] = jnp.zeros((EDGE, width), padded.dtype)
    blocks = [(stack, i) for stack in stacks for i in range(stack.shape[0])]
    for number, (stack, i) in enumerate(blocks):
        own = stack.shape[1]
        at = pl.multiple_of(EDGE + places[number] * own, 32)
        padded[pl.ds(at, own)] = stack[i]
    for piece in filtered:
        piece[rows:] = jnp.zeros((EDGE, width), piece.dtype)
    dot = functools.partial(jnp.dot, preferred_element_type=jnp.float32)
    for start in range(0, rows, BLOCK):
        same = arc_rows[start : start + BLOCK] == arc_behind[:, start : start + wide]
        window = padded[start : start + wide]
        total = jnp.zeros((BLOCK, width), jnp.float32)
        for piece in split(jnp.where(same, forward, 0.0), 3)[::-1]:
            total = total + dot(piece, window)
        for ref, piece in zip(filtered, split(total, 3), strict=True):
            ref[start : start + BLOCK] = piece
    per = rows // groups // 16
    for start in range(0, rows, BLOCK):
        same = arc_rows[start : start + BLOCK] == arc_ahead[:, start : start + wide]
        pieces = split(jnp.where(same, backward, 0.0), 3)
        total = jnp.zeros((BLOCK, width), jnp.float32)
        for i, j in ((2, 0), (1, 1), (0, 2), (1, 0), (0, 1), (0, 0)):
            total = total + dot(pieces[i], filtered[j][start : start + wide])
        total = total.astype(out.dtype)
        for tile in range(BLOCK // 16):
            group, spot = divmod(start // 16 + tile, per)
            at = (spot * groups + group) * 16
            out[at : at + 16] = total[tile * 16 : tile * 16 + 16]


SMEM = pl.BlockSpec(memory_space=pltpu.SMEM)
VMEM = pl.BlockSpec(memory_space=pltpu.VMEM)


def weighted(places, stacks, taps, arc_id, groups):
    width = stacks[0].shape[-1]
    rows = arc_id.shape[0]
    arc_behind = jnp.pad(arc_id, (EDGE, 128 - EDGE), constant_values=-1)[None]
    arc_ahead = jnp.pad(arc_id, (0, 128), constant_values=-1)[None]
    return pl.pallas_call(
        functools.partial(weigh, groups),
        out_shape=jax.ShapeDtypeStruct((rows, width), jnp.bfloat16),
        in_specs=[SMEM, SMEM] + [VMEM] * (3 + len(stacks)),
        out_specs=VMEM,
        scratch_shapes=[pltpu.VMEM((rows + EDGE, width), jnp.bfloat16)] * 4,
        compiler_params=pltpu.CompilerParams(vmem_limit_bytes=12 << 20),
        cost_estimate=pl.CostEstimate(
            flops=18 * rows * (BLOCK + EDGE) * width,
            bytes_accessed=4 * rows * width,
            transcendentals=0,
        ),
    )(places, taps, arc_id[:, None], arc_ahead, arc_behind, *stacks)


def accumulate(count, sides, carried, at, *refs):
    weights, refs = refs[:sides], refs[sides:]
    blocks, refs = refs[:count], refs[count:]
    priors, outs, left = refs[:carried], refs[carried : carried + sides], refs[-1]
    half = weights[0].shape[0] // 24

    @pl.when(pl.program_id(0) == 0)
    def _():
        for side in range(sides):
            picked = []
            for number in range(left.shape[2] // half):
                rows = pl.ds(pl.multiple_of(at[number] * half, half), half)
                picked.append(weights[side][rows])
            left[side] = jnp.concatenate(picked, axis=0).T

    right = jnp.concatenate([block[...] for block in blocks], axis=0)
    for side in range(sides):
        total = jnp.dot(left[side], right, preferred_element_type=jnp.float32)
        for prior in priors[side::sides]:
            total = total + prior[...]
        outs[side][...] = total


def product(at, weights, blocks, priors, tile):
    sides = len(weights)
    depth = sum(block.shape[0] for block in blocks)
    columns = blocks[0].shape[1]
    width = weights[0].shape[1]
    spec = pl.BlockSpec((width, tile), lambda i: (0, i))
    return pl.pallas_call(
        functools.partial(accumulate, len(blocks), sides, len(priors)),
        out_shape=[jax.ShapeDtypeStruct((width, columns), jnp.float32)] * sides,
        grid=(columns // tile,),
        in_specs=[SMEM]
        + [VMEM] * sides
        + [pl.BlockSpec((b.shape[0], tile), lambda i: (0, i)) for b in blocks]
        + [spec] * len(priors),
        out_specs=[spec] * sides,
        scratch_shapes=[pltpu.VMEM((sides, width, depth), jnp.bfloat16)],
        compiler_params=pltpu.CompilerParams(vmem_limit_bytes=14 << 20),
        cost_estimate=pl.CostEstimate(
            flops=2 * sides * width * depth * columns,
            bytes_accessed=2 * depth * columns + 4 * (sides + len(priors)) * width * columns,
            transcendentals=0,
        ),
    )(at, *weights, *blocks, *priors)


def block_of(static_design, tv_design, taps, arc_id):
    turns = lax.axis_size("ring")
    half = turns // 2
    ring, core = lax.axis_index("ring"), lax.axis_index("core")
    swap = [(0, 1), (1, 0)]
    onward = [(2 * i, (i + 1) % turns * 2) for i in range(turns)]
    onward += [((i + 1) % turns * 2 + 1, i * 2 + 1) for i in range(turns)]

    def hop(block):
        return lax.ppermute(block, ("ring", "core"), onward)

    other = lax.ppermute(static_design, "col_1", swap)
    mine = [lax.all_gather(tv_design, "short", axis=0, tiled=True)]
    theirs = [lax.ppermute(mine[0], "core", swap)]

    pair = jnp.stack([static_design, other])
    beside = lax.ppermute(pair, "col_0", [(i, i ^ 1) for i in range(4)])
    opposite = lax.ppermute(jnp.concatenate([pair, beside]), "col_0", [(i, 3 - i) for i in range(4)])
    places = (lax.axis_index("col_0") ^ jnp.array([0, 0, 1, 1, 3, 3, 2, 2], jnp.int32)) * 2
    places = places + (lax.axis_index("col_1") ^ jnp.array([0, 1] * 4, jnp.int32))

    for _ in range(1, half):
        mine.append(hop(mine[-1]))
        theirs.append(hop(theirs[-1]))
    mine.append(hop(mine[-1]))

    left = weighted(places, (pair, beside, opposite), taps, arc_id, lax.axis_size("short"))
    lefts = (left, lax.ppermute(left, "core", swap))

    def chosen(blocks):
        part = jnp.array([part for part, _ in blocks], jnp.int32)
        steps = jnp.array([steps for _, steps in blocks], jnp.int32)
        origin = (ring + turns + jnp.where(core == 0, -steps, steps)) % turns
        return origin * 2 + (core + part) % 2

    def near(blocks, priors):
        tv = [(mine, theirs)[part][steps] for part, steps in blocks]
        return product(chosen(blocks), lefts, tv, priors, 1024)

    sums = near([(0, d) for d in range(4)] + [(1, d) for d in range(1, 4)], ())
    sums = near([(0, 4), (1, 4), (0, 5)], sums)
    handed = lax.ppermute(sums[1], "core", swap)
    far = [lax.all_gather(theirs[half - 1], "core", axis=0, tiled=True)]
    far.append(lax.all_gather(mine[half], "core", axis=0, tiled=True))
    steps = jnp.array([1 - half, half - 1, -half, half], jnp.int32)
    at = (ring + turns + steps) % turns * 2 + jnp.array([1, 0, 0, 1], jnp.int32)
    return product(at, lefts[:1], far, (sums[0], handed), 1024)[0]


def solution(mesh):
    finer = Mesh(
        mesh.devices.reshape(4, 12, 2, 4, 2),
        ("short", "ring", "core", "col_0", "col_1"),
    )
    row = ("short", "ring", "core")
    placed = (P(COL, row), P(row, COL), P(), P())
    return jax.shard_map(
        block_of, mesh=finer, in_specs=placed, out_specs=P(row, COL), check_vma=False
    )
```

```python
import functools

import jax
import jax.numpy as jnp
from jax import lax
from jax.experimental import pallas as pl
from jax.experimental.pallas import tpu as pltpu
from jax.sharding import Mesh
from jax.sharding import PartitionSpec as P

BLOCK = 192
EDGE = 32
COL = ("col_0", "col_1")


def split(values, parts):
    pieces = []
    for _ in range(parts):
        piece = values.astype(jnp.bfloat16)
        pieces.append(piece)
        values = values - piece.astype(jnp.float32)
    return pieces


def banded(taps, lag):
    band = jnp.zeros(lag.shape, jnp.float32)
    for step in range(taps.shape[0]):
        band = jnp.where(lag == step, taps[step], band)
    return band


def weigh(groups, spot, taps, arc_id, *refs):
    stacks, (out, arcs, padded, *filtered) = refs[:3], refs[3:]
    rows, width = out.shape
    wide = BLOCK + EDGE
    down = lax.broadcasted_iota(jnp.int32, (BLOCK, wide), 0)
    across = lax.broadcasted_iota(jnp.int32, (BLOCK, wide), 1)
    forward = banded(taps, down + EDGE - across)
    backward = banded(taps, across - down)

    arcs[...] = jnp.full(arcs.shape, -1, jnp.int32)
    arcs[:, EDGE : EDGE + rows] = arc_id[...]

    def arc_column(start):
        row = arcs[:, start + EDGE : start + EDGE + 256]
        return jnp.broadcast_to(row, (8, 256)).T[:BLOCK, :1]

    padded[:EDGE] = jnp.zeros((EDGE, width), padded.dtype)
    blocks = [(stack, i) for stack in stacks for i in range(stack.shape[0])]
    for number, (stack, i) in enumerate(blocks):
        own = stack.shape[1]
        place = (spot[2] ^ (0, 1, 3, 2)[number // 2]) * 2 + (spot[3] ^ (number % 2))
        at = pl.multiple_of(EDGE + place * own, 32)
        padded[pl.ds(at, own)] = stack[i]
    for piece in filtered:
        piece[rows:] = jnp.zeros((EDGE, width), piece.dtype)
    dot = functools.partial(jnp.dot, preferred_element_type=jnp.float32)
    for start in range(0, rows, BLOCK):
        same = arc_column(start) == arcs[:, start : start + wide]
        window = padded[start : start + wide]
        total = jnp.zeros((BLOCK, width), jnp.float32)
        for piece in split(jnp.where(same, forward, 0.0), 3)[::-1]:
            total = total + dot(piece, window)
        for ref, piece in zip(filtered, split(total, 3), strict=True):
            ref[start : start + BLOCK] = piece
    per = rows // groups // 16
    for start in range(0, rows, BLOCK):
        same = arc_column(start) == arcs[:, start + EDGE : start + EDGE + wide]
        pieces = split(jnp.where(same, backward, 0.0), 3)
        total = jnp.zeros((BLOCK, width), jnp.float32)
        for i, j in ((2, 0), (1, 1), (0, 2), (1, 0), (0, 1), (0, 0)):
            total = total + dot(pieces[i], filtered[j][start : start + wide])
        total = total.astype(out.dtype)
        for tile in range(BLOCK // 16):
            group, spot = divmod(start // 16 + tile, per)
            at = (spot * groups + group) * 16
            out[at : at + 16] = total[tile * 16 : tile * 16 + 16]


SMEM = pl.BlockSpec(memory_space=pltpu.SMEM)
VMEM = pl.BlockSpec(memory_space=pltpu.VMEM)


def weighted(spot, stacks, taps, arc_id, groups):
    width = stacks[0].shape[-1]
    rows = arc_id.shape[0]
    return pl.pallas_call(
        functools.partial(weigh, groups),
        out_shape=jax.ShapeDtypeStruct((rows, width), jnp.bfloat16),
        in_specs=[SMEM, SMEM] + [VMEM] * (1 + len(stacks)),
        out_specs=VMEM,
        scratch_shapes=[pltpu.VMEM((1, rows + 128), jnp.int32)]
        + [pltpu.VMEM((rows + EDGE, width), jnp.bfloat16)] * 4,
        compiler_params=pltpu.CompilerParams(vmem_limit_bytes=12 << 20),
        cost_estimate=pl.CostEstimate(
            flops=18 * rows * (BLOCK + EDGE) * width,
            bytes_accessed=4 * rows * width,
            transcendentals=0,
        ),
    )(spot, taps, arc_id[None], *stacks)


def accumulate(count, sides, carried, met, spot, *refs):
    weights, refs = refs[:sides], refs[sides:]
    blocks, refs = refs[:count], refs[count:]
    priors, outs, left = refs[:carried], refs[carried : carried + sides], refs[-1]
    half = weights[0].shape[0] // 24
    ring, core = spot[0], spot[1]

    @pl.when(pl.program_id(0) == 0)
    def _():
        starts = []
        for part, steps, fixed in met:
            turn = 12 + steps if fixed else jnp.where(core == 0, 12 - steps, 12 + steps)
            origin = lax.rem(ring + turn, 12)
            which = part if fixed else core ^ part
            starts.append(pl.multiple_of((origin * 2 + which) * half, half))
        for side in range(sides):
            picked = [weights[side][pl.ds(start, half)] for start in starts]
            left[side] = jnp.concatenate(picked, axis=0).T

    right = jnp.concatenate([block[...] for block in blocks], axis=0)
    for side in range(sides):
        total = jnp.dot(left[side], right, preferred_element_type=jnp.float32)
        for prior in priors[side::sides]:
            total = total + prior[...].astype(jnp.float32)
        outs[side][...] = total.astype(outs[side].dtype)


def product(spot, weights, blocks, met, priors, kinds, tile):
    sides = len(weights)
    depth = sum(block.shape[0] for block in blocks)
    columns = blocks[0].shape[1]
    width = weights[0].shape[1]
    spec = pl.BlockSpec((width, tile), lambda i: (0, i))
    return pl.pallas_call(
        functools.partial(accumulate, len(blocks), sides, len(priors), tuple(met)),
        out_shape=[jax.ShapeDtypeStruct((width, columns), kind) for kind in kinds],
        grid=(columns // tile,),
        in_specs=[SMEM]
        + [VMEM] * sides
        + [pl.BlockSpec((b.shape[0], tile), lambda i: (0, i)) for b in blocks]
        + [spec] * len(priors),
        out_specs=[spec] * sides,
        scratch_shapes=[pltpu.VMEM((sides, width, depth), jnp.bfloat16)],
        compiler_params=pltpu.CompilerParams(vmem_limit_bytes=14 << 20),
        cost_estimate=pl.CostEstimate(
            flops=2 * sides * width * depth * columns,
            bytes_accessed=2 * depth * columns + 4 * (sides + len(priors)) * width * columns,
            transcendentals=0,
        ),
    )(spot, *weights, *blocks, *priors)


def block_of(static_design, tv_design, taps, arc_id):
    turns = lax.axis_size("ring")
    half = turns // 2
    swap = [(0, 1), (1, 0)]
    onward = [(2 * i, (i + 1) % turns * 2) for i in range(turns)]
    onward += [((i + 1) % turns * 2 + 1, i * 2 + 1) for i in range(turns)]

    def hop(block):
        return lax.ppermute(block, ("ring", "core"), onward)

    other = lax.ppermute(static_design, "col_1", swap)
    mine = [lax.all_gather(tv_design, "short", axis=0, tiled=True)]
    theirs = [lax.ppermute(mine[0], "core", swap)]

    pair = jnp.stack([static_design, other])
    beside = lax.ppermute(pair, "col_0", [(i, i ^ 1) for i in range(4)])
    opposite = lax.ppermute(jnp.concatenate([pair, beside]), "col_0", [(i, 3 - i) for i in range(4)])
    spot = jnp.stack([lax.axis_index(axis) for axis in ("ring", "core") + COL])

    for _ in range(1, half):
        mine.append(hop(mine[-1]))
        theirs.append(hop(theirs[-1]))
    mine.append(hop(mine[-1]))

    left = weighted(spot, (pair, beside, opposite), taps, arc_id, lax.axis_size("short"))
    lefts = (left, lax.ppermute(left, "core", swap))

    def near(blocks, priors, kinds):
        tv = [(mine, theirs)[part][steps] for part, steps in blocks]
        met = [(part, steps, False) for part, steps in blocks]
        return product(spot, lefts, tv, met, priors, kinds, 1024)

    f32 = jnp.float32
    first = [(0, d) for d in range(4)] + [(1, d) for d in range(1, 4)]
    sums = near(first, (), (f32, f32))
    sums = near([(0, 4), (1, 4), (0, 5)], sums, (f32, jnp.bfloat16))
    handed = lax.ppermute(sums[1], "core", swap)
    far = [lax.all_gather(theirs[half - 1], "core", axis=0, tiled=True)]
    far.append(lax.all_gather(mine[half], "core", axis=0, tiled=True))
    met = [(1, 1 - half, True), (0, half - 1, True), (0, -half, True), (1, half, True)]
    return product(spot, lefts[:1], far, met, (sums[0], handed), (f32,), 1024)[0]


def solution(mesh):
    finer = Mesh(
        mesh.devices.reshape(4, 12, 2, 4, 2),
        ("short", "ring", "core", "col_0", "col_1"),
    )
    row = ("short", "ring", "core")
    placed = (P(COL, row), P(row, COL), P(), P())
    return jax.shard_map(
        block_of, mesh=finer, in_specs=placed, out_specs=P(row, COL), check_vma=False
    )
```

```python
import functools

import jax
import jax.numpy as jnp
from jax import lax
from jax.experimental import pallas as pl
from jax.experimental.pallas import tpu as pltpu
from jax.sharding import Mesh
from jax.sharding import PartitionSpec as P

BLOCK = 192
EDGE = 32
COL = ("col_0", "col_1")


def split(values, parts):
    pieces = []
    for _ in range(parts):
        piece = values.astype(jnp.bfloat16)
        pieces.append(piece)
        values = values - piece.astype(jnp.float32)
    return pieces


def banded(taps, lag):
    band = jnp.zeros(lag.shape, jnp.float32)
    for step in range(taps.shape[0]):
        band = jnp.where(lag == step, taps[step], band)
    return band


def weigh(groups, spot, taps, arc_rows, arcs, *refs):
    stacks, (out, padded, *filtered) = refs[:3], refs[3:]
    rows, width = out.shape
    wide = BLOCK + EDGE
    down = lax.broadcasted_iota(jnp.int32, (BLOCK, wide), 0)
    across = lax.broadcasted_iota(jnp.int32, (BLOCK, wide), 1)
    forward = banded(taps, down + EDGE - across)
    backward = banded(taps, across - down)

    padded[:EDGE] = jnp.zeros((EDGE, width), padded.dtype)
    blocks = [(stack, i) for stack in stacks for i in range(stack.shape[0])]
    for number, (stack, i) in enumerate(blocks):
        own = stack.shape[1]
        place = (spot[2] ^ (0, 1, 3, 2)[number // 2]) * 2 + (spot[3] ^ (number % 2))
        at = pl.multiple_of(EDGE + place * own, 32)
        padded[pl.ds(at, own)] = stack[i]
    for piece in filtered:
        piece[rows:] = jnp.zeros((EDGE, width), piece.dtype)
    dot = functools.partial(jnp.dot, preferred_element_type=jnp.float32)
    for start in range(0, rows, BLOCK):
        same = arc_rows[start : start + BLOCK] == arcs[:, start : start + wide]
        window = padded[start : start + wide]
        total = jnp.zeros((BLOCK, width), jnp.float32)
        for piece in split(jnp.where(same, forward, 0.0), 3)[::-1]:
            total = total + dot(piece, window)
        for ref, piece in zip(filtered, split(total, 3), strict=True):
            ref[start : start + BLOCK] = piece
    per = rows // groups // 16
    for start in range(0, rows, BLOCK):
        same = arc_rows[start : start + BLOCK] == arcs[:, start + EDGE : start + EDGE + wide]
        pieces = split(jnp.where(same, backward, 0.0), 3)
        total = jnp.zeros((BLOCK, width), jnp.float32)
        for i, j in ((2, 0), (1, 1), (0, 2), (1, 0), (0, 1), (0, 0)):
            total = total + dot(pieces[i], filtered[j][start : start + wide])
        total = total.astype(out.dtype)
        for tile in range(BLOCK // 16):
            group, spot = divmod(start // 16 + tile, per)
            at = (spot * groups + group) * 16
            out[at : at + 16] = total[tile * 16 : tile * 16 + 16]


SMEM = pl.BlockSpec(memory_space=pltpu.SMEM)
VMEM = pl.BlockSpec(memory_space=pltpu.VMEM)


def weighted(spot, stacks, taps, arc_id, groups):
    width = stacks[0].shape[-1]
    rows = arc_id.shape[0]
    arcs = jnp.pad(arc_id, (EDGE, 128 - EDGE), constant_values=-1)[None]
    arc_rows = arc_id[:, None]
    return pl.pallas_call(
        functools.partial(weigh, groups),
        out_shape=jax.ShapeDtypeStruct((rows, width), jnp.bfloat16),
        in_specs=[SMEM, SMEM] + [VMEM] * (2 + len(stacks)),
        out_specs=VMEM,
        scratch_shapes=[pltpu.VMEM((rows + EDGE, width), jnp.bfloat16)] * 4,
        compiler_params=pltpu.CompilerParams(vmem_limit_bytes=12 << 20),
        cost_estimate=pl.CostEstimate(
            flops=18 * rows * (BLOCK + EDGE) * width,
            bytes_accessed=4 * rows * width,
            transcendentals=0,
        ),
    )(spot, taps, arc_rows, arcs, *stacks)


def accumulate(count, sides, carried, met, spot, *refs):
    weights, refs = refs[:sides], refs[sides:]
    blocks, refs = refs[:count], refs[count:]
    priors, outs, left = refs[:carried], refs[carried : carried + sides], refs[-1]
    half = weights[0].shape[0] // 24
    ring, core = spot[0], spot[1]

    @pl.when(pl.program_id(0) == 0)
    def _():
        starts = []
        for part, steps, fixed in met:
            turn = 12 + steps if fixed else jnp.where(core == 0, 12 - steps, 12 + steps)
            origin = lax.rem(ring + turn, 12)
            which = part if fixed else core ^ part
            starts.append(pl.multiple_of((origin * 2 + which) * half, half))
        for side in range(sides):
            picked = [weights[side][pl.ds(start, half)] for start in starts]
            left[side] = jnp.concatenate(picked, axis=0).T

    right = jnp.concatenate([block[...] for block in blocks], axis=0)
    for side in range(sides):
        total = jnp.dot(left[side], right, preferred_element_type=jnp.float32)
        for prior in priors[side::sides]:
            total = total + prior[...].astype(jnp.float32)
        outs[side][...] = total.astype(outs[side].dtype)


def product(spot, weights, blocks, met, priors, kinds, tile):
    sides = len(weights)
    depth = sum(block.shape[0] for block in blocks)
    columns = blocks[0].shape[1]
    width = weights[0].shape[1]
    spec = pl.BlockSpec((width, tile), lambda i: (0, i))
    return pl.pallas_call(
        functools.partial(accumulate, len(blocks), sides, len(priors), tuple(met)),
        out_shape=[jax.ShapeDtypeStruct((width, columns), kind) for kind in kinds],
        grid=(columns // tile,),
        in_specs=[SMEM]
        + [VMEM] * sides
        + [pl.BlockSpec((b.shape[0], tile), lambda i: (0, i)) for b in blocks]
        + [spec] * len(priors),
        out_specs=[spec] * sides,
        scratch_shapes=[pltpu.VMEM((sides, width, depth), jnp.bfloat16)],
        compiler_params=pltpu.CompilerParams(vmem_limit_bytes=14 << 20),
        cost_estimate=pl.CostEstimate(
            flops=2 * sides * width * depth * columns,
            bytes_accessed=2 * depth * columns + 4 * (sides + len(priors)) * width * columns,
            transcendentals=0,
        ),
    )(spot, *weights, *blocks, *priors)


def block_of(static_design, tv_design, taps, arc_id):
    turns = lax.axis_size("ring")
    half = turns // 2
    swap = [(0, 1), (1, 0)]
    onward = [(2 * i, (i + 1) % turns * 2) for i in range(turns)]
    onward += [((i + 1) % turns * 2 + 1, i * 2 + 1) for i in range(turns)]

    def hop(block):
        return lax.ppermute(block, ("ring", "core"), onward)

    other = lax.ppermute(static_design, "col_1", swap)
    mine = [lax.all_gather(tv_design, "short", axis=0, tiled=True)]
    theirs = [lax.ppermute(mine[0], "core", swap)]

    pair = jnp.stack([static_design, other])
    beside = lax.ppermute(pair, "col_0", [(i, i ^ 1) for i in range(4)])
    opposite = lax.ppermute(jnp.concatenate([pair, beside]), "col_0", [(i, 3 - i) for i in range(4)])
    spot = jnp.stack([lax.axis_index(axis) for axis in ("ring", "core") + COL])

    for _ in range(1, half):
        mine.append(hop(mine[-1]))
        theirs.append(hop(theirs[-1]))
    mine.append(hop(mine[-1]))

    left = weighted(spot, (pair, beside, opposite), taps, arc_id, lax.axis_size("short"))
    lefts = (left, lax.ppermute(left, "core", swap))

    def near(blocks, priors, kinds):
        tv = [(mine, theirs)[part][steps] for part, steps in blocks]
        met = [(part, steps, False) for part, steps in blocks]
        return product(spot, lefts, tv, met, priors, kinds, 1024)

    f32 = jnp.float32
    first = [(0, d) for d in range(4)] + [(1, d) for d in range(1, 4)]
    sums = near(first, (), (f32, f32))
    sums = near([(0, 4), (1, 4), (0, 5)], sums, (f32, jnp.bfloat16))
    handed = lax.ppermute(sums[1], "core", swap)
    far = [lax.all_gather(theirs[half - 1], "core", axis=0, tiled=True)]
    far.append(lax.all_gather(mine[half], "core", axis=0, tiled=True))
    met = [(1, 1 - half, True), (0, half - 1, True), (0, -half, True), (1, half, True)]
    return product(spot, lefts[:1], far, met, (sums[0], handed), (f32,), 1024)[0]


def solution(mesh):
    finer = Mesh(
        mesh.devices.reshape(4, 12, 2, 4, 2),
        ("short", "ring", "core", "col_0", "col_1"),
    )
    row = ("short", "ring", "core")
    placed = (P(COL, row), P(row, COL), P(), P())
    return jax.shard_map(
        block_of, mesh=finer, in_specs=placed, out_specs=P(row, COL), check_vma=False
    )
```
